32 devices in a mesh: shot: 4 (over y, x), blk: 8 (over z, core).
Axes of the slice: x: 2, y: 2, z: 4, core: 2. Of those that a mesh axis runs over, the one named last changes fastest.
Arguments:
- intensities: bfloat16 [2048, 16, 128], P('blk', 'shot'), may hold values from -6 to 6
- tile_owner: int32 [2048], P('blk'), may hold values from 0 to 7, as said below
- tile_place: int32 [2048], P('blk'), may hold values from 0 to 255
- tile_kernel: int32 [2048], P('blk'), may hold values from 0 to 3
- mask_len: int32 [2048], P('blk'), may hold values from 1 to 128
- interp_weights: bfloat16 [4, 128, 128], replicated, may hold values from 0 to 1.2
Outputs:
- corr_diff: float32 [16, 128, 2048], P('shot', 'blk')
The draws below stay inside these ranges and needn't reach their ends.
Inputs may be any that keep to these rules, and one draw needn't show every extreme that they name: `tile_owner`: in each device's block of 256 tiles no owner is named by more than 96 tiles, and one owner, the same for every block, is named by exactly 96 tiles of every block.
All inputs are finite; a program needn't handle non-finite values.
Results may differ from the reference program's by a relative error of at most 0.0003.
Values may be sent and summed in bfloat16 or wider, within the bound.
No kernel may reach another device: no remote copies, remote signals or barrier semaphores. Data moves between devices by JAX's collectives and lax.ppermute only.
A program may use at most 64 MiB of HBM per device.

```python
import math
import jax
import jax.numpy as jnp
import numpy as np
from jax import lax

ANG = 2048
TP = 128
Q_DEV = 16
KERN = 4
TILES_DEV = 256
NSEG = 16
OWNERS = 8
Q = 128
CAP = 96
TILES = 2048
SHOTS = 16


def draw_tile_owner(key, part):
    hot_owner = jax.random.randint(jax.random.fold_in(key, 11), (), 0, OWNERS)
    others = jnp.arange((OWNERS - 1) * CAP, dtype=jnp.int32) // CAP
    others = others + (others >= hot_owner).astype(jnp.int32)

    def one_block(block_key):
        first_key, second_key = jax.random.split(block_key)
        selected_index = jax.random.permutation(first_key, others)[:TILES_DEV - CAP]
        filled = jnp.concatenate([jnp.full((CAP,), hot_owner, jnp.int32), selected_index])
        return jax.random.permutation(second_key, filled)
    block_keys = jax.random.split(jax.random.fold_in(key, 13), OWNERS)
    return jax.vmap(one_block)(block_keys).reshape(-1).astype(jnp.int32)


def draw_interp_weights(key, part):
    diag_key, off_key = jax.random.split(jax.random.fold_in(key, 17))
    diagonal = jax.random.uniform(diag_key, (KERN, TP), jnp.float32, 0.5, 1.0)
    spread = jax.random.uniform(off_key, (KERN, TP, TP), jnp.float32, 0.0, 0.6 / TP)
    identity = jnp.eye(TP, dtype=jnp.float32)
    return (spread * (1.0 - identity)[None] + identity[None] * diagonal[:, None, :]).astype(jnp.bfloat16)


def set_ends(array, rng, least, largest):
    spot = [jax.random.randint(jax.random.fold_in(rng, axis), (), 0, length) for axis, length in enumerate(array.shape)]
    longest = array.shape.index(max(array.shape))
    next_to = spot[:longest] + [(spot[longest] + 1) % array.shape[longest]] + spot[longest + 1:]
    return array.at[tuple(spot)].set(least).at[tuple(next_to)].set(largest)


def shard_levels(own_key, shape, cuts, low, largest):
    level, own = 1.0, jax.random.fold_in(own_key, 6)
    for position, shards_of in cuts:
        draws = jnp.exp(jax.random.uniform(jax.random.fold_in(own, position), (shards_of,), jnp.float32, low / len(cuts), largest / len(cuts)))
        level = level * jnp.repeat(draws, shape[position] // shards_of).reshape([-1 if axis == position else 1 for axis in range(len(shape))])
    return level


def cumulative_ranks(amount, skew):
    portions = [(1 << 20) // math.isqrt(grade ** skew) + 1 for grade in range(1, amount + 1)]
    width = 1 + sum(portions) // (1 << 30)
    return np.cumsum(np.array([max(1, weight // width) for weight in portions]))


def ranked_ids(key, shape, amount, slope):
    table = cumulative_ranks(amount, slope)
    ticket = jax.random.randint(jax.random.fold_in(key, 1), shape, 0, int(table[amount - 1]))
    rank = jnp.searchsorted(jnp.asarray(table, jnp.int32), ticket, side="right")
    return jax.random.permutation(jax.random.fold_in(key, 2), amount)[rank].astype(jnp.int32)


def normal_values(key, shape, width, limit, shards=(), kind=jnp.bfloat16):
    values = width * jax.random.normal(key, shape, jnp.float32)
    if shards:
        values = values * shard_levels(key, shape, shards, -0.22, 0.18)
    return jnp.clip(values, -limit, limit).astype(kind)


def setup_inputs(seed: int = 0) -> dict:
    splits = jax.random.split(jax.random.key(seed), 7)
    intensities = normal_values(splits[0], (TILES, SHOTS, TP), 1.0, 6.0, ((0, 8), (1, 4)))
    tile_owner = draw_tile_owner(jax.random.fold_in(splits[6], 71), 0)
    tile_place = set_ends(ranked_ids(splits[2], (TILES,), Q_DEV * NSEG, 3), jax.random.fold_in(splits[2], 3), 0, (Q_DEV * NSEG) - 1).astype(jnp.int32)
    tile_kernel = set_ends(jax.random.randint(splits[3], (TILES,), 0, KERN), jax.random.fold_in(splits[3], 1), 0, KERN - 1).astype(jnp.int32)
    mask_len = set_ends(jax.random.randint(splits[4], (TILES,), 1, TP + 1), jax.random.fold_in(splits[4], 1), 1, TP).astype(jnp.int32)
    interp_weights = draw_interp_weights(jax.random.fold_in(splits[6], 71), 0)
    return {"intensities": intensities, "tile_owner": tile_owner, "tile_place": tile_place, "tile_kernel": tile_kernel, "mask_len": mask_len, "interp_weights": interp_weights}


def reference(intensities, tile_owner, tile_place, tile_kernel, mask_len, interp_weights):
    slot_count = Q_DEV * NSEG
    weights = interp_weights.astype(jnp.float32)
    pixel_index = jnp.arange(TP, dtype=jnp.int32)
    blocks = (
        intensities.reshape(OWNERS, TILES_DEV, SHOTS, TP),
        tile_owner.reshape(OWNERS, TILES_DEV),
        tile_place.reshape(OWNERS, TILES_DEV),
        tile_kernel.reshape(OWNERS, TILES_DEV),
        mask_len.reshape(OWNERS, TILES_DEV),
    )

    def block_step(running, block_data):
        pixels, owners, places, kernels, lengths = block_data
        live_values = (pixel_index[None, :] < lengths[:, None]).astype(jnp.float32)
        selected_rows = jnp.take(weights, kernels, axis=0)
        masked_intensity = pixels.astype(jnp.float32) * live_values[:, None, :]
        value_entries = jnp.einsum("tsp,tpa->tsa", masked_intensity, selected_rows, precision=lax.Precision.HIGHEST)
        mask_values = jnp.einsum("tp,tpa->ta", live_values, selected_rows, precision=lax.Precision.HIGHEST)
        slot_ids = (owners * slot_count + places).astype(jnp.int32)
        total_values = running[0] + jax.ops.segment_sum(value_entries, slot_ids, num_segments=OWNERS * slot_count)
        total_masks = running[1] + jax.ops.segment_sum(mask_values, slot_ids, num_segments=OWNERS * slot_count)
        return (total_values, total_masks), None

    start = (
        jnp.zeros((OWNERS * slot_count, SHOTS, TP), jnp.float32),
        jnp.zeros((OWNERS * slot_count, TP), jnp.float32),
    )
    finals = lax.scan(block_step, start, blocks)[0]
    cycle_int = finals[0].reshape(Q, NSEG, SHOTS, TP).transpose(2, 0, 1, 3).reshape(SHOTS, Q, ANG)
    cycle_mask = finals[1].reshape(Q, ANG)
    next_int = jnp.roll(cycle_int, -1, axis=0)
    spectrum = jnp.fft.fft(cycle_int, axis=-1)
    next_spectrum = jnp.fft.fft(next_int, axis=-1)
    auto_corr = jnp.real(jnp.fft.ifft(spectrum * jnp.conj(spectrum), axis=-1))
    cross_corr = jnp.real(jnp.fft.ifft(spectrum * jnp.conj(next_spectrum), axis=-1))
    mask_spectrum = jnp.fft.fft(cycle_mask, axis=-1)
    mask_corr = jnp.real(jnp.fft.ifft(mask_spectrum * jnp.conj(mask_spectrum), axis=-1))
    denominator = jnp.maximum(jnp.maximum(mask_corr, 0.01 * mask_corr[:, :1]), 1.0)
    return ((auto_corr - cross_corr) / denominator[None]).astype(jnp.float32)
```

```python
import math

import jax
import jax.numpy as jnp
import ml_dtypes
import numpy as np
from jax import lax
from jax.experimental import pallas as pl
from jax.experimental.pallas import tpu as pltpu
from jax.sharding import PartitionSpec as P

ANG = 2048
TP = 128
Q_DEV = 16
NSEG = 16
LANES = 128
META = 8


F32 = jnp.float32
BF16 = jnp.bfloat16


def halves(array):
    high = array.astype(np.float32).astype(ml_dtypes.bfloat16)
    low = (array - high.astype(np.float64)).astype(np.float32).astype(ml_dtypes.bfloat16)
    return np.stack([high, low])


def tables():
    half = NSEG // 2 + 1
    k1 = np.arange(half)
    seg = np.arange(NSEG)
    turn = 2.0 * np.pi * np.outer(k1, seg) / NSEG
    same = np.eye(Q_DEV)
    slots = Q_DEV * NSEG
    first = np.stack([np.cos(turn), -np.sin(turn)])
    first = np.einsum("pks,qr->pkqrs", first, same).reshape(2 * half * Q_DEV, slots)
    weight = np.where((k1 == 0) | (2 * k1 == NSEG), 1.0, 2.0) / ANG
    last = np.stack([np.cos(turn) * weight[:, None], -np.sin(turn) * weight[:, None]])
    last = np.einsum("pks,qr->sqpkr", last, same).reshape(slots, 2 * half * Q_DEV)
    lane = np.arange(TP)
    angle = 2.0 * np.pi * (np.outer(lane, lane) % TP) / TP
    cosine, sine = np.cos(angle), np.sin(angle)
    forward = np.block([[cosine, -sine], [sine, cosine]])
    inverse = np.block([[cosine, sine], [-sine, cosine]])
    twist = 2.0 * np.pi * np.outer(k1, lane) / ANG
    twist = np.repeat(np.stack([np.cos(twist), np.sin(twist)]), Q_DEV, axis=1)
    return halves(first), halves(last), halves(forward), halves(inverse), twist.astype(np.float32)


def split(value):
    high = value.astype(BF16)
    return high, (value - high.astype(F32)).astype(BF16)


def dot(a, b):
    return jnp.dot(a, b, preferred_element_type=F32)


def dot_rows(a, b):
    return lax.dot_general(a, b, (((1,), (1,)), ((), ())), preferred_element_type=F32)


def table_dot(table_ref, value):
    high, low = split(value)
    return dot(table_ref[0], high) + (dot(table_ref[0], low) + dot(table_ref[1], high))


def dot_table(value, table_high, table_low):
    high, low = split(value)
    return dot(high, table_high) + (dot(high, table_low) + dot(low, table_high))


def iota(shape, axis):
    return lax.broadcasted_iota(jnp.int32, shape, axis)


def pack_kernel(owners, capacity, me_ref, owner_ref, place_ref, kern_ref, len_ref, pix_ref, *rest):
    outs, wide = rest[:owners], rest[owners]
    tiles = owner_ref.shape[1]
    shots = pix_ref.shape[0] // tiles
    wide[...] = pix_ref[...].astype(F32)
    pixels = jnp.concatenate(
        [wide[pl.ds(s, tiles, stride=shots), :].astype(BF16) for s in range(shots)], axis=1
    )
    owner = owner_ref[...]
    mine = (iota((owners, tiles), 0) == owner).astype(F32)
    before = (iota((tiles, tiles), 0) < iota((tiles, tiles), 1)).astype(F32).astype(BF16)
    rank = jnp.sum(dot(mine.astype(BF16), before) * mine, axis=0, keepdims=True)
    slot = (owner ^ me_ref[0]) * LANES + rank.astype(jnp.int32)
    meta = jnp.concatenate(
        [
            place_ref[...].astype(F32),
            (kern_ref[...] + 1).astype(F32),
            len_ref[...].astype(F32),
            jnp.zeros((META - 3, tiles), F32),
        ],
        axis=0,
    ).astype(BF16)
    for d in range(owners):
        placing = (iota((LANES, tiles), 0) + d * LANES == slot).astype(F32).astype(BF16)
        sent = dot(placing[:capacity], pixels).astype(BF16)
        for s in range(shots):
            outs[d][s * capacity : (s + 1) * capacity, :] = sent[:, s * TP : (s + 1) * TP]
        outs[d][shots * capacity :, :] = dot_rows(meta, placing).astype(BF16)


def gather_kernel(owners, capacity, *refs):
    got = refs[:owners]
    weights_ref, cyc0_ref, cyc_ref, table = refs[owners:]
    kernels = weights_ref.shape[0]
    slots = Q_DEV * NSEG
    shots = (got[0].shape[0] - META) // capacity
    metas = [g[shots * capacity :, :].astype(F32) for g in got]
    group = math.gcd(owners, 8)
    for base in range(0, owners, group):
        lens = jnp.concatenate([m[2:3] for m in metas[base : base + group]], axis=0)
        lens = jnp.transpose(lens)
        for i in range(group):
            d = base + i
            live = iota((capacity, TP), 1).astype(F32) < lens[:capacity, i : i + 1]
            for s in range(shots):
                pix = got[d][s * capacity : (s + 1) * capacity, :].astype(F32)
                table[d * LANES : d * LANES + capacity, s * TP : (s + 1) * TP] = jnp.where(
                    live, pix, 0.0
                ).astype(BF16)
            table[d * LANES : d * LANES + capacity, shots * TP :] = jnp.where(
                live, 1.0, 0.0
            ).astype(BF16)
            if capacity < LANES:
                table[d * LANES + capacity : (d + 1) * LANES, :] = jnp.zeros(
                    (LANES - capacity, (shots + 1) * TP), BF16
                )
    pick = []
    for m in metas:
        index = jnp.where(m[1:2] > 0.5, m[0:1] + (m[1:2] - 1.0) * slots, -1.0)
        hit = iota((kernels * slots, LANES), 0) == index.astype(jnp.int32)
        pick.append(hit.astype(F32).astype(BF16))
    sums = dot(jnp.concatenate(pick, axis=1), table[...])
    weights = weights_ref[...].reshape(kernels * TP, TP)
    for s in range(shots + 1):
        high, low = split(
            jnp.concatenate(
                [
                    sums[k * slots : (k + 1) * slots, s * TP : (s + 1) * TP]
                    for k in range(kernels)
                ],
                axis=1,
            )
        )
        cycle = dot(high, weights) + dot(low, weights)
        if s == 0:
            cyc0_ref[...] = cycle
        else:
            cyc_ref[:, (s - 1) * TP : s * TP] = cycle


def spectrum(cycles, first_ref, forward_ref, twist_ref):
    rows = table_dot(first_ref, cycles)
    half = rows.shape[0] // 2
    cosine, sine = twist_ref[0], twist_ref[1]
    turned = []
    for s in range(cycles.shape[1] // TP):
        real = rows[:half, s * TP : (s + 1) * TP]
        imag = rows[half:, s * TP : (s + 1) * TP]
        turned.append(
            jnp.concatenate(
                [real * cosine + imag * sine, imag * cosine - real * sine], axis=1
            )
        )
    return dot_table(jnp.concatenate(turned, axis=0), forward_ref[0], forward_ref[1])


def untwist(grid, twist_ref):
    cosine, sine = twist_ref[0], twist_ref[1]
    real, imag = grid[:, :TP], grid[:, TP:]
    return jnp.concatenate(
        [real * cosine - imag * sine, real * sine + imag * cosine], axis=0
    )


def forward_kernel(cyc0_ref, cyc_ref, first_ref, last_ref, forward_ref, inverse_ref, twist_ref,
                   spec_ref, scale_ref):
    half = twist_ref.shape[1]
    cycles = jnp.concatenate([cyc0_ref[...], cyc_ref[...]], axis=1)
    spec = spectrum(cycles, first_ref, forward_ref, twist_ref)
    own = spec_ref.shape[0]
    spec_ref[...] = spec[:own]
    real, imag = spec[own:, :TP], spec[own:, TP:]
    power = real * real + imag * imag
    grid = dot_table(power, inverse_ref[0, :TP, :], inverse_ref[1, :TP, :])
    corr = table_dot(last_ref, untwist(grid, twist_ref))
    least = jnp.maximum(0.01 * corr[:Q_DEV, :1], 1.0)
    for m in range(NSEG):
        part = corr[m * Q_DEV : (m + 1) * Q_DEV, :]
        scale_ref[m * Q_DEV : (m + 1) * Q_DEV, :] = 1.0 / jnp.maximum(part, least)


def correlate_kernel(next_ref, spec_ref, scale_ref, first_ref, last_ref, forward_ref, inverse_ref,
                     twist_ref, out_ref):
    half = twist_ref.shape[1]
    after = spectrum(next_ref[...], first_ref, forward_ref, twist_ref)
    spec = spec_ref[...]
    shots = spec.shape[0] // half
    diff = spec - jnp.concatenate([spec[half:], after], axis=0)
    real, imag = spec[:, :TP], spec[:, TP:]
    diff_real, diff_imag = diff[:, :TP], diff[:, TP:]
    cross = jnp.concatenate(
        [real * diff_real + imag * diff_imag, imag * diff_real - real * diff_imag], axis=1
    )
    grid = dot_table(cross, inverse_ref[0], inverse_ref[1])
    turned = jnp.concatenate(
        [untwist(grid[s * half : (s + 1) * half], twist_ref) for s in range(shots)], axis=1
    )
    corr = table_dot(last_ref, turned)
    for s in range(shots):
        for m in range(NSEG):
            rows = slice(m * Q_DEV, (m + 1) * Q_DEV)
            out_ref[s, :, m * TP : (m + 1) * TP] = (
                corr[rows, s * TP : (s + 1) * TP] * scale_ref[rows, :]
            )


VMEM = pl.BlockSpec(memory_space=pltpu.VMEM)
SMEM = pl.BlockSpec(memory_space=pltpu.SMEM)


def call(body, outs, operands, scratch=(), scalars=0, cost=0):
    return pl.pallas_call(
        body,
        out_shape=outs,
        in_specs=[SMEM] * scalars + [VMEM] * (len(operands) - scalars),
        out_specs=jax.tree.map(lambda _: VMEM, outs),
        scratch_shapes=list(scratch),
        cost_estimate=pl.CostEstimate(flops=cost, bytes_accessed=1 << 20, transcendentals=0),
    )(*operands)


def per_device(intensities, tile_owner, tile_place, tile_kernel, mask_len, interp_weights):
    owners = lax.axis_size("blk")
    tiles, shots, _ = intensities.shape
    capacity = -(-(3 * tiles // owners) // 16) * 16
    slots = Q_DEV * NSEG
    half_rows = (NSEG // 2 + 1) * Q_DEV
    first, last, forward, inverse, twist = (jnp.asarray(t) for t in tables())
    me = lax.axis_index("blk").astype(jnp.int32).reshape(1)
    rows = shots * capacity + META
    sent = call(
        lambda *refs: pack_kernel(owners, capacity, *refs),
        [jax.ShapeDtypeStruct((rows, TP), BF16)] * owners,
        [
            me,
            tile_owner.reshape(1, tiles),
            tile_place.reshape(1, tiles),
            tile_kernel.reshape(1, tiles),
            mask_len.reshape(1, tiles),
            intensities.reshape(tiles * shots, TP),
        ],
        scratch=[pltpu.VMEM((tiles * shots, TP), F32)],
        scalars=1,
    )
    got = [sent[0]] + [
        lax.ppermute(sent[d], "blk", [(i, i ^ d) for i in range(owners)])
        for d in reversed(range(1, owners))
    ]
    cyc0, cyc = call(
        lambda *refs: gather_kernel(owners, capacity, *refs),
        [
            jax.ShapeDtypeStruct((slots, TP), F32),
            jax.ShapeDtypeStruct((slots, shots * TP), F32),
        ],
        [*got, interp_weights],
        scratch=[pltpu.VMEM((owners * LANES, (shots + 1) * TP), BF16)],
    )
    ring = lax.axis_size("shot")
    after = lax.ppermute(cyc0, "shot", [((i + 1) % ring, i) for i in range(ring)])
    spec, scale = call(
        forward_kernel,
        [
            jax.ShapeDtypeStruct((shots * half_rows, 2 * TP), F32),
            jax.ShapeDtypeStruct((slots, TP), F32),
        ],
        [cyc0, cyc, first, last, forward, inverse, twist],
        cost=10**9,
    )
    return call(
        correlate_kernel,
        jax.ShapeDtypeStruct((shots, Q_DEV, ANG), F32),
        [after, spec, scale, first, last, forward, inverse, twist],
    )


def solution(mesh):
    owners = mesh.shape["blk"]
    assert owners & (owners - 1) == 0
    placed = (P("blk", "shot", None), P("blk"), P("blk"), P("blk"), P("blk"), P())
    return jax.shard_map(
        per_device, mesh=mesh, in_specs=placed, out_specs=P("shot", "blk", None), check_vma=False
    )
```

```python
import math

import jax
import jax.numpy as jnp
import ml_dtypes
import numpy as np
from jax import lax
from jax.experimental import pallas as pl
from jax.experimental.pallas import tpu as pltpu
from jax.sharding import PartitionSpec as P

ANG = 2048
TP = 128
Q_DEV = 16
NSEG = 16
LANES = 128
META = 8


F32 = jnp.float32
BF16 = jnp.bfloat16


def halves(array):
    high = array.astype(np.float32).astype(ml_dtypes.bfloat16)
    low = (array - high.astype(np.float64)).astype(np.float32).astype(ml_dtypes.bfloat16)
    return np.stack([high, low])


def tables():
    half = NSEG // 2 + 1
    k1 = np.arange(half)
    seg = np.arange(NSEG)
    turn = 2.0 * np.pi * np.outer(k1, seg) / NSEG
    same = np.eye(Q_DEV)
    slots = Q_DEV * NSEG
    first = np.stack([np.cos(turn), -np.sin(turn)])
    first = np.einsum("pks,qr->pkqrs", first, same).reshape(2 * half * Q_DEV, slots)
    weight = np.where((k1 == 0) | (2 * k1 == NSEG), 1.0, 2.0) / ANG
    last = np.stack([np.cos(turn) * weight[:, None], -np.sin(turn) * weight[:, None]])
    last = np.einsum("pks,qr->sqpkr", last, same).reshape(slots, 2 * half * Q_DEV)
    lane = np.arange(TP)
    angle = 2.0 * np.pi * (np.outer(lane, lane) % TP) / TP
    cosine, sine = np.cos(angle), np.sin(angle)
    forward = np.block([[cosine, -sine], [sine, cosine]])
    inverse = np.block([[cosine, sine], [-sine, cosine]])
    twist = 2.0 * np.pi * np.outer(k1, lane) / ANG
    twist = np.repeat(np.stack([np.cos(twist), np.sin(twist)]), Q_DEV, axis=1)
    return halves(first), halves(last), halves(forward), halves(inverse), twist.astype(np.float32)


def split(value):
    high = value.astype(BF16)
    return high, (value - high.astype(F32)).astype(BF16)


def dot(a, b):
    return jnp.dot(a, b, preferred_element_type=F32)


def dot_rows(a, b):
    return lax.dot_general(a, b, (((1,), (1,)), ((), ())), preferred_element_type=F32)


def table_dot(table_ref, value):
    high, low = split(value)
    return dot(table_ref[0], high) + (dot(table_ref[0], low) + dot(table_ref[1], high))


def dot_table(value, table_high, table_low):
    high, low = split(value)
    return dot(high, table_high) + (dot(high, table_low) + dot(low, table_high))


def iota(shape, axis):
    return lax.broadcasted_iota(jnp.int32, shape, axis)


def pack_kernel(owners, capacity, me_ref, owner_ref, place_ref, kern_ref, len_ref, pix_ref, *rest):
    outs, wide = rest[:owners], rest[owners]
    tiles = owner_ref.shape[1]
    shots = pix_ref.shape[0] // tiles
    wide[...] = pix_ref[...].astype(F32)
    pixels = jnp.concatenate(
        [wide[pl.ds(s, tiles, stride=shots), :].astype(BF16) for s in range(shots)], axis=1
    )
    owner = owner_ref[...]
    mine = (iota((owners, tiles), 0) == owner).astype(F32)
    before = (iota((tiles, tiles), 0) < iota((tiles, tiles), 1)).astype(F32).astype(BF16)
    rank = jnp.sum(dot(mine.astype(BF16), before) * mine, axis=0, keepdims=True)
    slot = (owner ^ me_ref[0]) * LANES + rank.astype(jnp.int32)
    meta = jnp.concatenate(
        [
            place_ref[...].astype(F32),
            (kern_ref[...] + 1).astype(F32),
            len_ref[...].astype(F32),
            jnp.zeros((META - 3, tiles), F32),
        ],
        axis=0,
    ).astype(BF16)
    for d in range(owners):
        placing = (iota((LANES, tiles), 0) + d * LANES == slot).astype(F32).astype(BF16)
        sent = dot(placing[:capacity], pixels).astype(BF16)
        for s in range(shots):
            outs[d][s * capacity : (s + 1) * capacity, :] = sent[:, s * TP : (s + 1) * TP]
        outs[d][shots * capacity :, :] = dot_rows(meta, placing).astype(BF16)


def gather_kernel(owners, capacity, *refs):
    got = refs[:owners]
    weights_ref, cyc0_ref, cyc_ref, table = refs[owners:]
    kernels = weights_ref.shape[0]
    slots = Q_DEV * NSEG
    shots = (got[0].shape[0] - META) // capacity
    metas = [g[shots * capacity :, :].astype(F32) for g in got]
    group = math.gcd(owners, 8)
    for base in range(0, owners, group):
        lens = jnp.concatenate([m[2:3] for m in metas[base : base + group]], axis=0)
        lens = jnp.transpose(lens)
        for i in range(group):
            d = base + i
            live = iota((capacity, TP), 1).astype(F32) < lens[:capacity, i : i + 1]
            for s in range(shots):
                pix = got[d][s * capacity : (s + 1) * capacity, :].astype(F32)
                table[d * LANES : d * LANES + capacity, s * TP : (s + 1) * TP] = jnp.where(
                    live, pix, 0.0
                ).astype(BF16)
            table[d * LANES : d * LANES + capacity, shots * TP :] = jnp.where(
                live, 1.0, 0.0
            ).astype(BF16)
            if capacity < LANES:
                table[d * LANES + capacity : (d + 1) * LANES, :] = jnp.zeros(
                    (LANES - capacity, (shots + 1) * TP), BF16
                )
    pick = []
    for m in metas:
        index = jnp.where(m[1:2] > 0.5, m[0:1] + (m[1:2] - 1.0) * slots, -1.0)
        hit = iota((kernels * slots, LANES), 0) == index.astype(jnp.int32)
        pick.append(hit.astype(F32).astype(BF16))
    sums = dot(jnp.concatenate(pick, axis=1), table[...])
    weights = weights_ref[...].reshape(kernels * TP, TP)
    for s in range(shots + 1):
        high, low = split(
            jnp.concatenate(
                [
                    sums[k * slots : (k + 1) * slots, s * TP : (s + 1) * TP]
                    for k in range(kernels)
                ],
                axis=1,
            )
        )
        cycle = dot(high, weights) + dot(low, weights)
        if s == 0:
            cyc0_ref[...] = cycle
        else:
            cyc_ref[:, (s - 1) * TP : s * TP] = cycle


def spectrum(cycles, first_ref, forward_ref, twist_ref):
    rows = table_dot(first_ref, cycles)
    half = rows.shape[0] // 2
    cosine, sine = twist_ref[0], twist_ref[1]
    turned = []
    for s in range(cycles.shape[1] // TP):
        real = rows[:half, s * TP : (s + 1) * TP]
        imag = rows[half:, s * TP : (s + 1) * TP]
        turned.append(
            jnp.concatenate(
                [real * cosine + imag * sine, imag * cosine - real * sine], axis=1
            )
        )
    return dot_table(jnp.concatenate(turned, axis=0), forward_ref[0], forward_ref[1])


def untwist(grid, twist_ref):
    cosine, sine = twist_ref[0], twist_ref[1]
    real, imag = grid[:, :TP], grid[:, TP:]
    return jnp.concatenate(
        [real * cosine - imag * sine, real * sine + imag * cosine], axis=0
    )


def forward_kernel(cyc0_ref, cyc_ref, first_ref, last_ref, forward_ref, inverse_ref, twist_ref,
                   spec_ref, scale_ref):
    half = twist_ref.shape[1]
    cycles = jnp.concatenate([cyc0_ref[...], cyc_ref[...]], axis=1)
    spec = spectrum(cycles, first_ref, forward_ref, twist_ref)
    own = spec_ref.shape[0]
    spec_ref[...] = spec[:own]
    real, imag = spec[own:, :TP], spec[own:, TP:]
    power = real * real + imag * imag
    grid = dot_table(power, inverse_ref[0, :TP, :], inverse_ref[1, :TP, :])
    corr = table_dot(last_ref, untwist(grid, twist_ref))
    least = jnp.maximum(0.01 * corr[:Q_DEV, :1], 1.0)
    for m in range(NSEG):
        part = corr[m * Q_DEV : (m + 1) * Q_DEV, :]
        scale_ref[m * Q_DEV : (m + 1) * Q_DEV, :] = 1.0 / jnp.maximum(part, least)


def correlate_kernel(next_ref, spec_ref, scale_ref, first_ref, last_ref, forward_ref, inverse_ref,
                     twist_ref, out_ref):
    half = twist_ref.shape[1]
    after = spectrum(next_ref[...], first_ref, forward_ref, twist_ref)
    spec = spec_ref[...]
    shots = spec.shape[0] // half
    diff = spec - jnp.concatenate([spec[half:], after], axis=0)
    real, imag = spec[:, :TP], spec[:, TP:]
    diff_real, diff_imag = diff[:, :TP], diff[:, TP:]
    cross = jnp.concatenate(
        [real * diff_real + imag * diff_imag, imag * diff_real - real * diff_imag], axis=1
    )
    grid = dot_table(cross, inverse_ref[0], inverse_ref[1])
    turned = jnp.concatenate(
        [untwist(grid[s * half : (s + 1) * half], twist_ref) for s in range(shots)], axis=1
    )
    corr = table_dot(last_ref, turned)
    for s in range(shots):
        for m in range(NSEG):
            rows = slice(m * Q_DEV, (m + 1) * Q_DEV)
            out_ref[s, :, m * TP : (m + 1) * TP] = (
                corr[rows, s * TP : (s + 1) * TP] * scale_ref[rows, :]
            )


VMEM = pl.BlockSpec(memory_space=pltpu.VMEM)
SMEM = pl.BlockSpec(memory_space=pltpu.SMEM)


def call(body, outs, operands, scratch=(), scalars=0, cost=0):
    return pl.pallas_call(
        body,
        out_shape=outs,
        in_specs=[SMEM] * scalars + [VMEM] * (len(operands) - scalars),
        out_specs=jax.tree.map(lambda _: VMEM, outs),
        scratch_shapes=list(scratch),
        compiler_params=pltpu.CompilerParams(vmem_limit_bytes=20 << 20),
        cost_estimate=pl.CostEstimate(flops=cost, bytes_accessed=1 << 20, transcendentals=0),
    )(*operands)


def per_device(intensities, tile_owner, tile_place, tile_kernel, mask_len, interp_weights):
    owners = lax.axis_size("blk")
    tiles, shots, _ = intensities.shape
    capacity = -(-(3 * tiles // owners) // 16) * 16
    slots = Q_DEV * NSEG
    half_rows = (NSEG // 2 + 1) * Q_DEV
    first, last, forward, inverse, twist = (jnp.asarray(t) for t in tables())
    me = lax.axis_index("blk").astype(jnp.int32).reshape(1)
    rows = shots * capacity + META
    sent = call(
        lambda *refs: pack_kernel(owners, capacity, *refs),
        [jax.ShapeDtypeStruct((rows, TP), BF16)] * owners,
        [
            me,
            tile_owner.reshape(1, tiles),
            tile_place.reshape(1, tiles),
            tile_kernel.reshape(1, tiles),
            mask_len.reshape(1, tiles),
            intensities.reshape(tiles * shots, TP),
        ],
        scratch=[pltpu.VMEM((tiles * shots, TP), F32)],
        scalars=1,
    )
    got = [sent[0]] + [
        lax.ppermute(sent[d], "blk", [(i, i ^ d) for i in range(owners)])
        for d in reversed(range(1, owners))
    ]
    cyc0, cyc = call(
        lambda *refs: gather_kernel(owners, capacity, *refs),
        [
            jax.ShapeDtypeStruct((slots, TP), F32),
            jax.ShapeDtypeStruct((slots, shots * TP), F32),
        ],
        [*got, interp_weights],
        scratch=[pltpu.VMEM((owners * LANES, (shots + 1) * TP), BF16)],
    )
    ring = lax.axis_size("shot")
    after = lax.ppermute(cyc0, "shot", [((i + 1) % ring, i) for i in range(ring)])
    spec, scale = call(
        forward_kernel,
        [
            jax.ShapeDtypeStruct((shots * half_rows, 2 * TP), F32),
            jax.ShapeDtypeStruct((slots, TP), F32),
        ],
        [cyc0, cyc, first, last, forward, inverse, twist],
        cost=10**9,
    )
    return call(
        correlate_kernel,
        jax.ShapeDtypeStruct((shots, Q_DEV, ANG), F32),
        [after, spec, scale, first, last, forward, inverse, twist],
    )


def solution(mesh):
    owners = mesh.shape["blk"]
    assert owners & (owners - 1) == 0
    placed = (P("blk", "shot", None), P("blk"), P("blk"), P("blk"), P("blk"), P())
    return jax.shard_map(
        per_device, mesh=mesh, in_specs=placed, out_specs=P("shot", "blk", None), check_vma=False
    )
```

```python
import math

import jax
import jax.numpy as jnp
import ml_dtypes
import numpy as np
from jax import lax
from jax.experimental import pallas as pl
from jax.experimental.pallas import tpu as pltpu
from jax.sharding import PartitionSpec as P


ANG = 2048
TP = 128
Q_DEV = 16
NSEG = 16
HALF = NSEG // 2 + 1
SLOTS = Q_DEV * NSEG
LANES = 128
META = 8
TWIST = 2 * 2 * TP
ROOT = math.sqrt(0.5)
COS1, SIN1 = math.cos(math.pi / 8), math.sin(math.pi / 8)


F32 = jnp.float32
BF16 = jnp.bfloat16


def pieces(array, count):
    terms = []
    for _ in range(count):
        terms.append(array.astype(np.float32).astype(ml_dtypes.bfloat16))
        array = array - terms[-1].astype(np.float64)
    return terms


def dft_table():
    lane = np.arange(TP)
    angle = 2.0 * np.pi * (np.outer(lane, lane) % TP) / TP
    cosine, sine = np.cos(angle), np.sin(angle)
    factors = np.block([[cosine, sine], [-sine, cosine]])
    turn = 2.0 * np.pi * np.outer(np.arange(NSEG), lane) / ANG
    twist = np.concatenate([np.cos(turn), np.sin(turn)], axis=1)
    return np.concatenate(pieces(factors, 2) + pieces(twist, 3), axis=0)


def split(value):
    high = value.astype(BF16)
    return high, (value - high.astype(F32)).astype(BF16)


def dot(a, b):
    return jnp.dot(a, b, preferred_element_type=F32)


def dot_rows(a, b):
    return lax.dot_general(a, b, (((1,), (1,)), ((), ())), preferred_element_type=F32)


def iota(shape, axis):
    return lax.broadcasted_iota(jnp.int32, shape, axis)


def factor_dot(value, table_ref):
    high, low = split(value)
    table_high, table_low = table_ref[: 2 * TP, :], table_ref[2 * TP : TWIST, :]
    return dot(high, table_high) + (dot(high, table_low) + dot(low, table_high))


def twist_of(table_ref):
    terms = [
        table_ref[TWIST + i * NSEG : TWIST + (i + 1) * NSEG, :].astype(F32) for i in range(3)
    ]
    whole = terms[0] + (terms[1] + terms[2])
    return [(whole[k : k + 1, :TP], whole[k : k + 1, TP:]) for k in range(HALF)]


def real_dft(x):
    a = [x[j] + x[j + 8] for j in range(8)]
    b = [x[j] - x[j + 8] for j in range(8)]
    c = [None] + [b[j] - b[8 - j] for j in range(1, 4)]
    s = [None] + [b[j] + b[8 - j] for j in range(1, 4)]
    a2 = [a[j] + a[j + 4] for j in range(4)]
    b2 = [a[j] - a[j + 4] for j in range(4)]
    real, imag = [None] * 9, [None] * 9
    even, odd = a2[0] + a2[2], a2[1] + a2[3]
    real[0], real[8] = even + odd, even - odd
    real[4], imag[4] = a2[0] - a2[2], a2[1] - a2[3]
    left, right = ROOT * (b2[1] - b2[3]), ROOT * (b2[1] + b2[3])
    real[2], real[6] = b2[0] + left, b2[0] - left
    imag[2], imag[6] = right + b2[2], right - b2[2]
    side, rise = ROOT * c[2], ROOT * s[2]
    for k, even, odd, odd_sine, even_sine in (
        (1, b[0] + side, COS1 * c[1] + SIN1 * c[3], SIN1 * s[1] + COS1 * s[3], rise + b[4]),
        (3, b[0] - side, SIN1 * c[1] - COS1 * c[3], COS1 * s[1] - SIN1 * s[3], rise - b[4]),
    ):
        real[k], real[8 - k] = even + odd, even - odd
        imag[k], imag[8 - k] = odd_sine + even_sine, odd_sine - even_sine
    return real, imag


def real_inverse(p, n):
    u1, v1, u3, v3 = p[1] + p[7], p[1] - p[7], p[3] + p[5], p[3] - p[5]
    x1, y1, x3, y3 = n[1] + n[7], n[1] - n[7], n[3] + n[5], n[3] - n[5]
    a = [u1 + u3, COS1 * v1 + SIN1 * v3, ROOT * (u1 - u3), SIN1 * v1 - COS1 * v3]
    b = [None, SIN1 * x1 + COS1 * x3, ROOT * (y1 + y3), COS1 * x1 - SIN1 * x3, y1 - y3]
    odd = [a[0], a[1] - b[1], a[2] - b[2], a[3] - b[3], -b[4]]
    odd += [-a[3] - b[3], -a[2] - b[2], -a[1] - b[1]]
    zero, eight = 0.5 * p[0], 0.5 * p[8]
    e0, e1 = zero + eight, zero - eight
    c, d = p[2] + p[6], ROOT * (p[2] - p[6])
    e, f = ROOT * (n[2] + n[6]), n[2] - n[6]
    up, down = e0 + p[4], e0 - p[4]
    left, right = e1 - n[4], e1 + n[4]
    near, far = d - e, d + e
    even = [up + c, left + near, down - f, right - far, up - c, left - near, down + f, right + far]
    return [even[m] + odd[m] for m in range(8)] + [even[m] - odd[m] for m in range(8)]


def slabs(value, count):
    return [value[k * Q_DEV : (k + 1) * Q_DEV, :] for k in range(count)]


def spectrum(cycles, table_ref):
    twist = twist_of(table_ref)
    reals, imags = [], []
    for cycle in cycles:
        real, imag = real_dft(slabs(cycle, NSEG))
        for k, (cosine, sine) in enumerate(twist):
            if k == 0:
                reals.append(real[k])
                imags.append(jnp.zeros_like(real[k]))
            elif imag[k] is None:
                reals.append(real[k] * cosine)
                imags.append(real[k] * sine)
            else:
                reals.append(real[k] * cosine - imag[k] * sine)
                imags.append(imag[k] * cosine + real[k] * sine)
    grid = jnp.concatenate(
        [jnp.concatenate(reals, axis=0), jnp.concatenate(imags, axis=0)], axis=1
    )
    return factor_dot(grid, table_ref)


def correlation(grid, twist):
    real, imag = slabs(grid[:, :TP], HALF), slabs(grid[:, TP:], HALF)
    p, n = [real[0]], [None]
    for k in range(1, HALF):
        cosine, sine = twist[k]
        p.append(real[k] * cosine - imag[k] * sine)
        n.append(None if k == HALF - 1 else real[k] * sine + imag[k] * cosine)
    return real_inverse(p, n)


def pack_kernel(owners, capacity, me_ref, owner_hbm, place_hbm, kern_hbm, len_hbm, pix_hbm, *rest):
    chips = owners // 2
    first, later = rest[:chips], rest[chips : 2 * chips]
    swap_first, swap_later, ints, pix, wide, sems = rest[2 * chips :]
    tiles = ints.shape[1]
    shots = pix.shape[0] // tiles
    first_rows, later_rows = capacity + META, (shots - 1) * capacity
    copies = [
        pltpu.make_async_copy(source, ints.at[pl.ds(8 * i, 1), :], sems.at[i])
        for i, source in enumerate((owner_hbm, place_hbm, kern_hbm, len_hbm))
    ]
    copies.append(pltpu.make_async_copy(pix_hbm, pix, sems.at[4]))
    for copy in copies:
        copy.start()
    before = (iota((tiles, tiles), 0) < iota((tiles, tiles), 1)).astype(F32).astype(BF16)
    for copy in copies[:4]:
        copy.wait()
    owner = ints[0:1, :]
    mine = (iota((owners, tiles), 0) == owner).astype(F32)
    rank = jnp.sum(dot(mine.astype(BF16), before) * mine, axis=0, keepdims=True)
    slot = (owner ^ me_ref[0]) * LANES + rank.astype(jnp.int32)
    place = ints[8:9, :]
    meta = jnp.concatenate(
        [
            ((place % NSEG) * Q_DEV + place // NSEG).astype(F32),
            (ints[16:17, :] + 1).astype(F32),
            ints[24:25, :].astype(F32),
            jnp.zeros((META - 3, tiles), F32),
        ],
        axis=0,
    ).astype(BF16)
    placing = [
        (iota((LANES, tiles), 0) + d * LANES == slot).astype(F32).astype(BF16)
        for d in range(owners)
    ]
    tags = [dot_rows(meta, placing[d]).astype(BF16) for d in range(owners)]
    copies[4].wait()
    wide[...] = pix[...].astype(F32)
    pixels = jnp.concatenate(
        [wide[pl.ds(s, tiles, stride=shots), :].astype(BF16) for s in range(shots)], axis=1
    )
    for d in range(owners):
        sent = dot(placing[d][:capacity], pixels).astype(BF16)
        j = d // 2
        if d % 2:
            near, far, at, to = swap_first, swap_later, j * first_rows, j * later_rows
        else:
            near, far, at, to = first[j], later[j], 0, 0
        near[at : at + capacity, :] = sent[:, :TP]
        near[at + capacity : at + first_rows, :] = tags[d]
        for s in range(1, shots):
            start = to + (s - 1) * capacity
            far[start : start + capacity, :] = sent[:, s * TP : (s + 1) * TP]


def merge_kernel(chips, *refs):
    own, other, outs = refs[: chips - 1], refs[chips - 1], refs[chips:]
    rows = own[0].shape[0]
    for j in range(1, chips):
        outs[j - 1][:rows, :] = own[j - 1][...]
        outs[j - 1][rows:, :] = other[j * rows : (j + 1) * rows, :]


def sources(own, other, far, rows):
    blocks = [own, other.at[pl.ds(0, rows), :]]
    for ref in far:
        blocks += [ref.at[pl.ds(0, rows), :], ref.at[pl.ds(rows, rows), :]]
    return blocks


def weigh(sums, count, weights_ref):
    kernels = weights_ref.shape[0]
    weights = weights_ref[...].reshape(kernels * TP, TP)
    cycles = []
    for s in range(count):
        columns = slice(s * TP, (s + 1) * TP)
        high, low = split(
            jnp.concatenate(
                [sums[k * SLOTS : (k + 1) * SLOTS, columns] for k in range(kernels)], axis=1
            )
        )
        cycles.append(dot(high, weights) + dot(low, weights))
    return cycles


def gather_kernel(owners, capacity, *refs):
    weights_hbm, pick_ref, live_ref, cyc0_ref, mask_ref, table, weights_ref, sem = refs[-8:]
    copy = pltpu.make_async_copy(weights_hbm, weights_ref, sem)
    copy.start()
    got = sources(refs[0], refs[1], refs[2:-8], capacity + META)
    kernels = weights_ref.shape[0]
    metas = [g[capacity : capacity + META, :].astype(F32) for g in got]
    group = math.gcd(owners, 8)
    for base in range(0, owners, group):
        lens = jnp.concatenate([m[2:3] for m in metas[base : base + group]], axis=0)
        lens = jnp.transpose(lens)
        for i in range(group):
            d = base + i
            rows = slice(d * capacity, (d + 1) * capacity)
            live = iota((capacity, TP), 1).astype(F32) < lens[:capacity, i : i + 1]
            live = jnp.where(live, 1.0, 0.0).astype(BF16)
            live_ref[rows, :] = live
            table[rows, :TP] = got[d][:capacity, :] * live
            table[rows, TP:] = live
    index = [
        jnp.where(m[1:2] > 0.5, m[0:1] + (m[1:2] - 1.0) * SLOTS, -1.0)[:, :capacity] for m in metas
    ]
    index = jnp.concatenate(index, axis=1).astype(jnp.int32)
    hit = iota((kernels * SLOTS, owners * capacity), 0) == index
    pick = hit.astype(F32).astype(BF16)
    pick_ref[...] = pick
    sums = dot(pick, table[...])
    copy.wait()
    cyc0_ref[...], mask_ref[...] = weigh(sums, 2, weights_ref)


def scale_kernel(cyc0_ref, mask_ref, table_ref, spec_ref, scale_ref):
    spec = spectrum([cyc0_ref[...], mask_ref[...]], table_ref)
    rows = spec_ref.shape[0]
    spec_ref[...] = spec[:rows]
    real, imag = spec[rows:, :TP], spec[rows:, TP:]
    power = jnp.concatenate([real * real + imag * imag, jnp.zeros_like(real)], axis=1)
    corr = correlation(factor_dot(power, table_ref), twist_of(table_ref))
    least = jnp.maximum(corr[0][:, :1] * (0.01 * 2.0 / ANG), 1.0)
    for m in range(NSEG):
        whole = jnp.maximum(corr[m] * (2.0 / ANG), least)
        scale_ref[m * Q_DEV : (m + 1) * Q_DEV, :] = (2.0 / ANG) / whole


def correlate_kernel(owners, capacity, *refs):
    (weights_ref, pick_ref, live_ref, spec_ref, next_ref, scale_ref, table_ref, out_hbm, table,
     out, sems) = refs[-11:]
    shots = out.shape[0]
    got = sources(refs[0], refs[1], refs[2:-11], (shots - 1) * capacity)
    for d in range(owners):
        rows = slice(d * capacity, (d + 1) * capacity)
        live = live_ref[rows, :]
        for s in range(shots - 1):
            table[rows, s * TP : (s + 1) * TP] = (
                got[d][s * capacity : (s + 1) * capacity, :] * live
            )
    cycles = weigh(dot(pick_ref[...], table[...]), shots - 1, weights_ref)
    spec = jnp.concatenate([spec_ref[...], spectrum(cycles + [next_ref[...]], table_ref)], axis=0)
    rows = HALF * Q_DEV
    diff = spec[: shots * rows] - spec[rows:]
    spec = spec[: shots * rows]
    real, imag = spec[:, :TP], spec[:, TP:]
    diff_real, diff_imag = diff[:, :TP], diff[:, TP:]
    cross = jnp.concatenate(
        [real * diff_real + imag * diff_imag, real * diff_imag - imag * diff_real], axis=1
    )
    grid = factor_dot(cross, table_ref)
    twist = twist_of(table_ref)
    copies = []
    for s in range(shots):
        corr = correlation(grid[s * rows : (s + 1) * rows], twist)
        for m in range(NSEG):
            out[s, :, m * TP : (m + 1) * TP] = corr[m] * scale_ref[m * Q_DEV : (m + 1) * Q_DEV, :]
        copies.append(pltpu.make_async_copy(out.at[s], out_hbm.at[s], sems.at[s]))
        copies[-1].start()
    for copy in copies:
        copy.wait()


VMEM = pl.BlockSpec(memory_space=pltpu.VMEM)
SMEM = pl.BlockSpec(memory_space=pltpu.SMEM)
HBM = pl.BlockSpec(memory_space=pltpu.HBM)


def call(body, outs, operands, in_specs=None, out_specs=None, scratch=(), flops=0, limit=20 << 20):
    return pl.pallas_call(
        body,
        out_shape=outs,
        in_specs=in_specs or [VMEM] * len(operands),
        out_specs=out_specs or jax.tree.map(lambda _: VMEM, outs),
        scratch_shapes=list(scratch),
        compiler_params=pltpu.CompilerParams(vmem_limit_bytes=limit),
        cost_estimate=pl.CostEstimate(flops=flops, bytes_accessed=1 << 20, transcendentals=0),
    )(*operands)


def far_order(owners):
    return sorted(range(2, owners, 2), key=lambda d: (d < owners // 2, -d))


def cross(block, d, owners):
    return lax.ppermute(block, "blk", [(i, i ^ d) for i in range(owners)])


def exchange(own, swap, owners):
    chips = owners // 2
    other = cross(swap, 1, owners)
    rows = own[0].shape[0]
    merged = call(
        lambda *refs: merge_kernel(chips, *refs),
        [jax.ShapeDtypeStruct((2 * rows, TP), BF16)] * (chips - 1),
        [*own[1:], other],
    )
    far = {d: cross(merged[d // 2 - 1], d, owners) for d in far_order(owners)}
    return [own[0], other] + [far[d] for d in range(2, owners, 2)]


def program(intensities, tile_owner, tile_place, tile_kernel, mask_len, interp_weights):
    owners = lax.axis_size("blk")
    chips = owners // 2
    ring = lax.axis_size("shot")
    tiles, shots, _ = intensities.shape
    kernels = interp_weights.shape[0]
    capacity = -(-(3 * tiles // owners) // 16) * 16
    rows = owners * capacity
    table = jnp.asarray(dft_table())
    me = lax.axis_index("blk").astype(jnp.int32).reshape(1)
    sent = call(
        lambda *refs: pack_kernel(owners, capacity, *refs),
        [jax.ShapeDtypeStruct((capacity + META, TP), BF16)] * chips
        + [jax.ShapeDtypeStruct(((shots - 1) * capacity, TP), BF16)] * chips
        + [jax.ShapeDtypeStruct((chips * (capacity + META), TP), BF16)]
        + [jax.ShapeDtypeStruct((chips * (shots - 1) * capacity, TP), BF16)],
        [
            me,
            *(
                pltpu.with_memory_space_constraint(v, pltpu.HBM)
                for v in (
                    tile_owner.reshape(1, tiles),
                    tile_place.reshape(1, tiles),
                    tile_kernel.reshape(1, tiles),
                    mask_len.reshape(1, tiles),
                    intensities.reshape(tiles * shots, TP),
                )
            ),
        ],
        in_specs=[SMEM] + [HBM] * 5,
        scratch=[
            pltpu.VMEM((32, tiles), jnp.int32),
            pltpu.VMEM((tiles * shots, TP), BF16),
            pltpu.VMEM((tiles * shots, TP), F32),
            pltpu.SemaphoreType.DMA((5,)),
        ],
    )
    early = exchange(sent[:chips], sent[2 * chips], owners)
    late = exchange(sent[chips : 2 * chips], sent[2 * chips + 1], owners)
    pick, live, cyc0, mask = call(
        lambda *refs: gather_kernel(owners, capacity, *refs),
        [
            jax.ShapeDtypeStruct((kernels * SLOTS, rows), BF16),
            jax.ShapeDtypeStruct((rows, TP), BF16),
            jax.ShapeDtypeStruct((SLOTS, TP), F32),
            jax.ShapeDtypeStruct((SLOTS, TP), F32),
        ],
        [*early, pltpu.with_memory_space_constraint(interp_weights, pltpu.HBM)],
        in_specs=[VMEM] * len(early) + [HBM],
        scratch=[
            pltpu.VMEM((rows, 2 * TP), BF16),
            pltpu.VMEM(interp_weights.shape, BF16),
            pltpu.SemaphoreType.DMA,
        ],
        flops=2 * 10**9,
    )
    after = lax.ppermute(cyc0, "shot", [((i + 1) % ring, i) for i in range(ring)])
    spec, scale = call(
        scale_kernel,
        [
            jax.ShapeDtypeStruct((HALF * Q_DEV, 2 * TP), F32),
            jax.ShapeDtypeStruct((SLOTS, TP), F32),
        ],
        [cyc0, mask, table],
        flops=10**9,
    )
    return call(
        lambda *refs: correlate_kernel(owners, capacity, *refs),
        jax.ShapeDtypeStruct((shots, Q_DEV, ANG), F32),
        [*late, interp_weights, pick, live, spec, after, scale, table],
        out_specs=HBM,
        scratch=[
            pltpu.VMEM((rows, (shots - 1) * TP), BF16),
            pltpu.VMEM((shots, Q_DEV, ANG), F32),
            pltpu.SemaphoreType.DMA((shots,)),
        ],
    )


def solution(mesh):
    owners = mesh.shape["blk"]
    assert owners & (owners - 1) == 0
    placed = (P("blk", "shot", None), P("blk"), P("blk"), P("blk"), P("blk"), P())
    return jax.shard_map(
        program, mesh=mesh, in_specs=placed, out_specs=P("shot", "blk", None), check_vma=False
    )
```

```python
import math

import jax
import jax.numpy as jnp
import ml_dtypes
import numpy as np
from jax import lax
from jax.experimental import pallas as pl
from jax.experimental.pallas import tpu as pltpu
from jax.sharding import PartitionSpec as P


ANG = 2048
TP = 128
Q_DEV = 16
NSEG = 16
HALF = NSEG // 2 + 1
SLOTS = Q_DEV * NSEG
LANES = 128
META = 8
LEAD = 2
TWIST = 2 * 2 * TP
ROOT = math.sqrt(0.5)
COS1, SIN1 = math.cos(math.pi / 8), math.sin(math.pi / 8)


F32 = jnp.float32
BF16 = jnp.bfloat16


def pieces(array, count):
    terms = []
    for _ in range(count):
        terms.append(array.astype(np.float32).astype(ml_dtypes.bfloat16))
        array = array - terms[-1].astype(np.float64)
    return terms


def dft_table():
    lane = np.arange(TP)
    angle = 2.0 * np.pi * (np.outer(lane, lane) % TP) / TP
    cosine, sine = np.cos(angle), np.sin(angle)
    factors = np.block([[cosine, sine], [-sine, cosine]])
    turn = 2.0 * np.pi * np.outer(np.arange(NSEG), lane) / ANG
    twist = np.concatenate([np.cos(turn), np.sin(turn)], axis=1)
    return np.concatenate(pieces(factors, 2) + pieces(twist, 3), axis=0)


def split(value):
    high = value.astype(BF16)
    return high, (value - high.astype(F32)).astype(BF16)


def dot(a, b):
    return jnp.dot(a, b, preferred_element_type=F32)


def dot_rows(a, b):
    return lax.dot_general(a, b, (((1,), (1,)), ((), ())), preferred_element_type=F32)


def iota(shape, axis):
    return lax.broadcasted_iota(jnp.int32, shape, axis)


def factor_dot(value, table_ref):
    high, low = split(value)
    table_high, table_low = table_ref[: 2 * TP, :], table_ref[2 * TP : TWIST, :]
    return dot(high, table_high) + (dot(high, table_low) + dot(low, table_high))


def twist_of(table_ref):
    terms = [
        table_ref[TWIST + i * NSEG : TWIST + (i + 1) * NSEG, :].astype(F32) for i in range(3)
    ]
    whole = terms[0] + (terms[1] + terms[2])
    return [(whole[k : k + 1, :TP], whole[k : k + 1, TP:]) for k in range(HALF)]


def real_dft(x):
    a = [x[j] + x[j + 8] for j in range(8)]
    b = [x[j] - x[j + 8] for j in range(8)]
    c = [None] + [b[j] - b[8 - j] for j in range(1, 4)]
    s = [None] + [b[j] + b[8 - j] for j in range(1, 4)]
    a2 = [a[j] + a[j + 4] for j in range(4)]
    b2 = [a[j] - a[j + 4] for j in range(4)]
    real, imag = [None] * 9, [None] * 9
    even, odd = a2[0] + a2[2], a2[1] + a2[3]
    real[0], real[8] = even + odd, even - odd
    real[4], imag[4] = a2[0] - a2[2], a2[1] - a2[3]
    left, right = ROOT * (b2[1] - b2[3]), ROOT * (b2[1] + b2[3])
    real[2], real[6] = b2[0] + left, b2[0] - left
    imag[2], imag[6] = right + b2[2], right - b2[2]
    side, rise = ROOT * c[2], ROOT * s[2]
    for k, even, odd, odd_sine, even_sine in (
        (1, b[0] + side, COS1 * c[1] + SIN1 * c[3], SIN1 * s[1] + COS1 * s[3], rise + b[4]),
        (3, b[0] - side, SIN1 * c[1] - COS1 * c[3], COS1 * s[1] - SIN1 * s[3], rise - b[4]),
    ):
        real[k], real[8 - k] = even + odd, even - odd
        imag[k], imag[8 - k] = odd_sine + even_sine, odd_sine - even_sine
    return real, imag


def real_inverse(p, n):
    u1, v1, u3, v3 = p[1] + p[7], p[1] - p[7], p[3] + p[5], p[3] - p[5]
    x1, y1, x3, y3 = n[1] + n[7], n[1] - n[7], n[3] + n[5], n[3] - n[5]
    a = [u1 + u3, COS1 * v1 + SIN1 * v3, ROOT * (u1 - u3), SIN1 * v1 - COS1 * v3]
    b = [None, SIN1 * x1 + COS1 * x3, ROOT * (y1 + y3), COS1 * x1 - SIN1 * x3, y1 - y3]
    odd = [a[0], a[1] - b[1], a[2] - b[2], a[3] - b[3], -b[4]]
    odd += [-a[3] - b[3], -a[2] - b[2], -a[1] - b[1]]
    zero, eight = 0.5 * p[0], 0.5 * p[8]
    e0, e1 = zero + eight, zero - eight
    c, d = p[2] + p[6], ROOT * (p[2] - p[6])
    e, f = ROOT * (n[2] + n[6]), n[2] - n[6]
    up, down = e0 + p[4], e0 - p[4]
    left, right = e1 - n[4], e1 + n[4]
    near, far = d - e, d + e
    even = [up + c, left + near, down - f, right - far, up - c, left - near, down + f, right + far]
    return [even[m] + odd[m] for m in range(8)] + [even[m] - odd[m] for m in range(8)]


def slabs(value, count):
    return [value[k * Q_DEV : (k + 1) * Q_DEV, :] for k in range(count)]


def spectrum(cycles, table_ref):
    twist = twist_of(table_ref)
    reals, imags = [], []
    for cycle in cycles:
        real, imag = real_dft(slabs(cycle, NSEG))
        for k, (cosine, sine) in enumerate(twist):
            if k == 0:
                reals.append(real[k])
                imags.append(jnp.zeros_like(real[k]))
            elif imag[k] is None:
                reals.append(real[k] * cosine)
                imags.append(real[k] * sine)
            else:
                reals.append(real[k] * cosine - imag[k] * sine)
                imags.append(imag[k] * cosine + real[k] * sine)
    grid = jnp.concatenate(
        [jnp.concatenate(reals, axis=0), jnp.concatenate(imags, axis=0)], axis=1
    )
    return factor_dot(grid, table_ref)


def correlation(grid, twist):
    real, imag = slabs(grid[:, :TP], HALF), slabs(grid[:, TP:], HALF)
    p, n = [real[0]], [None]
    for k in range(1, HALF):
        cosine, sine = twist[k]
        p.append(real[k] * cosine - imag[k] * sine)
        n.append(None if k == HALF - 1 else real[k] * sine + imag[k] * cosine)
    return real_inverse(p, n)


def pack_kernel(owners, capacity, me_ref, owner_hbm, place_hbm, kern_hbm, len_hbm, pix_hbm, *rest):
    chips = owners // 2
    first, later = rest[:chips], rest[chips : 2 * chips]
    swap_first, swap_later, lead, ints, pix, wide, sems = rest[2 * chips :]
    tiles = ints.shape[1]
    shots = pix.shape[0] // tiles
    first_rows, later_rows = capacity + META, (shots - 1) * capacity
    copies = [
        pltpu.make_async_copy(source, ints.at[pl.ds(8 * i, 1), :], sems.at[i])
        for i, source in enumerate((owner_hbm, place_hbm, kern_hbm, len_hbm))
    ]
    copies.append(pltpu.make_async_copy(pix_hbm, pix, sems.at[4]))
    for copy in copies:
        copy.start()
    before = (iota((tiles, tiles), 0) < iota((tiles, tiles), 1)).astype(F32).astype(BF16)
    for copy in copies[:4]:
        copy.wait()
    owner = ints[0:1, :]
    mine = (iota((owners, tiles), 0) == owner).astype(F32)
    rank = jnp.sum(dot(mine.astype(BF16), before) * mine, axis=0, keepdims=True)
    slot = (owner ^ me_ref[0]) * LANES + rank.astype(jnp.int32)
    place = ints[8:9, :]
    meta = jnp.concatenate(
        [
            ((place % NSEG) * Q_DEV + place // NSEG).astype(F32),
            (ints[16:17, :] + 1).astype(F32),
            ints[24:25, :].astype(F32),
            jnp.zeros((1, tiles), F32),
        ],
        axis=0,
    )
    blank = jnp.zeros_like(meta)
    metas = [
        jnp.concatenate(pair, axis=0).astype(BF16) for pair in ((meta, blank), (blank, meta))
    ]
    placing = [
        (iota((LANES, tiles), 0) + d * LANES == slot).astype(F32).astype(BF16)
        for d in range(owners)
    ]
    tags = [dot_rows(metas[d % 2], placing[d]).astype(BF16) for d in range(owners)]
    copies[4].wait()
    wide[...] = pix[...].astype(F32)
    pixels = jnp.concatenate(
        [wide[pl.ds(s, tiles, stride=shots), :].astype(BF16) for s in range(shots)], axis=1
    )
    for d in range(owners):
        sent = dot(placing[d][:capacity], pixels).astype(BF16)
        j = d // 2
        if d % 2:
            near, far, at, to = swap_first, swap_later, j * first_rows, j * later_rows
        else:
            near, far, at, to = first[j], later[j], 0, 0
        near[at : at + capacity, :] = sent[:, :TP]
        near[at + capacity : at + first_rows, :] = tags[d]
        for s in range(1, shots):
            start = to + (s - 1) * capacity
            out = far
            if d == owners // 2 and s >= shots - LEAD:
                out, start = lead, (s + LEAD - shots) * capacity
            out[start : start + capacity, :] = sent[:, s * TP : (s + 1) * TP]


def merge_kernel(chips, shared, *refs):
    own, other, outs = refs[: chips - 1], refs[chips - 1], refs[chips:]
    size = other.shape[0] // chips
    body = size - shared
    for j in range(1, chips):
        block, start, out = own[j - 1], j * size, outs[j - 1]
        first = block.shape[0] - shared
        out[:first, :] = block[:first, :]
        out[first : first + body, :] = other[start : start + body, :]
        if shared:
            out[first + body :, :] = block[first:, :] + other[start + body : start + size, :]


def interpolate(pixels, kern, weights_ref):
    kernels = weights_ref.shape[0]
    weights = jnp.concatenate([weights_ref[k] for k in range(kernels)], axis=1)
    every = dot(pixels, weights)
    value = every[:, :TP]
    for k in range(1, kernels):
        value = jnp.where(kern == k + 1.0, every[:, k * TP : (k + 1) * TP], value)
    return value


def scatter(pick, values):
    halves = [half for value in values for half in split(value)]
    sums = dot(pick, jnp.concatenate(halves, axis=1))
    return [
        sums[:, 2 * s * TP : (2 * s + 1) * TP] + sums[:, (2 * s + 1) * TP : (2 * s + 2) * TP]
        for s in range(len(values))
    ]


def gather_kernel(owners, capacity, *refs):
    weights_hbm, pick_ref, live_ref, kern_ref, cyc0_ref, mask_ref, weights_ref, sem = refs[-8:]
    copy = pltpu.make_async_copy(weights_hbm, weights_ref, sem)
    copy.start()
    got, metas = [], []
    for j in range(owners // 2):
        for core in range(2):
            ref = refs[core] if j == 0 else refs[j + 1]
            start = core * capacity if j else 0
            tags = ref[ref.shape[0] - META :, :] if j else ref[capacity : capacity + META, :]
            got.append(ref.at[pl.ds(start, capacity), :])
            metas.append(tags.astype(F32)[4 * core : 4 * core + 4])
    group = math.gcd(owners, 4)
    for base in range(0, owners, group):
        tags = jnp.concatenate([m[1:3] for m in metas[base : base + group]], axis=0)
        if group < 4:
            tags = jnp.concatenate([tags, jnp.zeros((8 - 2 * group, LANES), F32)], axis=0)
        tags = jnp.transpose(tags)
        for i in range(group):
            rows = slice((base + i) * capacity, (base + i + 1) * capacity)
            kern_ref[rows, :] = jnp.broadcast_to(
                tags[:capacity, 2 * i : 2 * i + 1], (capacity, TP)
            )
            live = iota((capacity, TP), 1).astype(F32) < tags[:capacity, 2 * i + 1 : 2 * i + 2]
            live_ref[rows, :] = jnp.where(live, 1.0, 0.0).astype(BF16)
    place = [jnp.where(m[1:2] > 0.5, m[0:1], -1.0)[:, :capacity] for m in metas]
    place = jnp.broadcast_to(jnp.concatenate(place, axis=1), (SLOTS, owners * capacity))
    slot = iota((SLOTS, owners * capacity), 0).astype(F32).astype(BF16)
    one = jnp.ones(slot.shape, BF16)
    pick_ref[...] = jnp.where(slot == place.astype(BF16), one, jnp.zeros_like(one))
    live, kern = live_ref[...], kern_ref[...]
    pixels = jnp.concatenate([g[...] for g in got], axis=0) * live
    copy.wait()
    cyc0_ref[...], mask_ref[...] = scatter(
        pick_ref[...],
        [interpolate(pixels, kern, weights_ref), interpolate(live, kern, weights_ref)],
    )


def scale_kernel(cyc0_ref, mask_ref, table_ref, spec_ref, scale_ref):
    spec = spectrum([cyc0_ref[...], mask_ref[...]], table_ref)
    rows = spec_ref.shape[0]
    spec_ref[...] = spec[:rows]
    real, imag = spec[rows:, :TP], spec[rows:, TP:]
    power = jnp.concatenate([real * real + imag * imag, jnp.zeros_like(real)], axis=1)
    corr = correlation(factor_dot(power, table_ref), twist_of(table_ref))
    least = jnp.maximum(corr[0][:, :1] * (0.01 * 2.0 / ANG), 1.0)
    for m in range(NSEG):
        whole = jnp.maximum(corr[m] * (2.0 / ANG), least)
        scale_ref[m * Q_DEV : (m + 1) * Q_DEV, :] = (2.0 / ANG) / whole


def late_blocks(far, capacity, shots, lead=None):
    blocks = []
    for ref in far:
        for core in range(2):
            start = core * (ref.shape[0] - shots * capacity)
            held = shots if lead is None or blocks else shots - LEAD
            block = [ref.at[pl.ds(start + s * capacity, capacity), :] for s in range(held)]
            block += [
                lead.at[pl.ds(s * capacity, capacity), :] for s in range(shots - held)
            ]
            blocks.append(block)
    return blocks


def late_cycles(blocks, live_ref, kern_ref, pick_ref, weights_ref, first):
    count = sum(ref.shape[0] for ref in blocks[0])
    capacity = count // len(blocks[0])
    rows = slice(first, first + capacity * len(blocks))
    live, kern = live_ref[rows, :], kern_ref[rows, :]
    values = [
        interpolate(
            jnp.concatenate([block[s][...] for block in blocks], axis=0) * live, kern, weights_ref
        )
        for s in range(len(blocks[0]))
    ]
    return scatter(pick_ref[:, rows], values)


def partial_kernel(capacity, shots, own, other, *refs):
    (weights_ref, pick_ref, live_ref, kern_ref, next_ref, table_ref, part_ref, spec_ref) = refs[-8:]
    blocks = [
        [ref.at[pl.ds(s * capacity, capacity), :] for s in range(shots)] for ref in (own, other)
    ]
    blocks += late_blocks(refs[:-8], capacity, shots)
    cycles = late_cycles(blocks, live_ref, kern_ref, pick_ref, weights_ref, 0)
    for s, cycle in enumerate(cycles):
        part_ref[:, s * TP : (s + 1) * TP] = cycle
    spec_ref[...] = spectrum([next_ref[...]], table_ref)


def correlate_kernel(capacity, lead, *refs):
    (weights_ref, pick_ref, live_ref, kern_ref, part_ref, spec_ref, next_ref, scale_ref, table_ref,
     out_hbm, out, sems) = refs[-12:]
    shots = out.shape[0]
    blocks = late_blocks(refs[:-12], capacity, shots - 1, lead)
    first = live_ref.shape[0] - capacity * len(blocks)
    cycles = late_cycles(blocks, live_ref, kern_ref, pick_ref, weights_ref, first)
    cycles = [c + part_ref[:, s * TP : (s + 1) * TP] for s, c in enumerate(cycles)]
    spec = jnp.concatenate([spec_ref[...], spectrum(cycles, table_ref), next_ref[...]], axis=0)
    rows = HALF * Q_DEV
    diff = spec[: shots * rows] - spec[rows:]
    spec = spec[: shots * rows]
    real, imag = spec[:, :TP], spec[:, TP:]
    diff_real, diff_imag = diff[:, :TP], diff[:, TP:]
    cross = jnp.concatenate(
        [real * diff_real + imag * diff_imag, real * diff_imag - imag * diff_real], axis=1
    )
    grid = factor_dot(cross, table_ref)
    twist = twist_of(table_ref)
    copies = []
    for s in range(shots):
        corr = correlation(grid[s * rows : (s + 1) * rows], twist)
        for m in range(NSEG):
            out[s, :, m * TP : (m + 1) * TP] = corr[m] * scale_ref[m * Q_DEV : (m + 1) * Q_DEV, :]
        copies.append(pltpu.make_async_copy(out.at[s], out_hbm.at[s], sems.at[s]))
        copies[-1].start()
    for copy in copies:
        copy.wait()


VMEM = pl.BlockSpec(memory_space=pltpu.VMEM)
SMEM = pl.BlockSpec(memory_space=pltpu.SMEM)
HBM = pl.BlockSpec(memory_space=pltpu.HBM)


def call(body, outs, operands, in_specs=None, out_specs=None, scratch=(), flops=0, limit=20 << 20):
    return pl.pallas_call(
        body,
        out_shape=outs,
        in_specs=in_specs or [VMEM] * len(operands),
        out_specs=out_specs or jax.tree.map(lambda _: VMEM, outs),
        scratch_shapes=list(scratch),
        compiler_params=pltpu.CompilerParams(vmem_limit_bytes=limit),
        cost_estimate=pl.CostEstimate(flops=flops, bytes_accessed=1 << 20, transcendentals=0),
    )(*operands)


def far_order(owners):
    return sorted(range(2, owners, 2), key=lambda d: (d < owners // 2, -d))


def cross(block, d, owners):
    return lax.ppermute(block, "blk", [(i, i ^ d) for i in range(owners)])


def exchange(own, swap, owners, shared):
    chips = owners // 2
    other = cross(swap, 1, owners)
    size = swap.shape[0] // chips - shared
    merged = call(
        lambda *refs: merge_kernel(chips, shared, *refs),
        [jax.ShapeDtypeStruct((block.shape[0] + size, TP), BF16) for block in own[1:]],
        [*own[1:], other],
    )
    far = {d: cross(merged[d // 2 - 1], d, owners) for d in far_order(owners)}
    return own[0], other, [far[d] for d in range(2, owners, 2)]


def program(intensities, tile_owner, tile_place, tile_kernel, mask_len, interp_weights):
    owners = lax.axis_size("blk")
    chips = owners // 2
    ring = lax.axis_size("shot")
    tiles, shots, _ = intensities.shape
    capacity = -(-(3 * tiles // owners) // 16) * 16
    rows = owners * capacity
    table = jnp.asarray(dft_table())
    me = lax.axis_index("blk").astype(jnp.int32).reshape(1)
    sent = call(
        lambda *refs: pack_kernel(owners, capacity, *refs),
        [jax.ShapeDtypeStruct((capacity + META, TP), BF16)] * chips
        + [
            jax.ShapeDtypeStruct(((shots - 1 - LEAD * (4 * j == owners)) * capacity, TP), BF16)
            for j in range(chips)
        ]
        + [jax.ShapeDtypeStruct((chips * (capacity + META), TP), BF16)]
        + [jax.ShapeDtypeStruct((chips * (shots - 1) * capacity, TP), BF16)]
        + [jax.ShapeDtypeStruct((LEAD * capacity, TP), BF16)],
        [
            me,
            *(
                pltpu.with_memory_space_constraint(v, pltpu.HBM)
                for v in (
                    tile_owner.reshape(1, tiles),
                    tile_place.reshape(1, tiles),
                    tile_kernel.reshape(1, tiles),
                    mask_len.reshape(1, tiles),
                    intensities.reshape(tiles * shots, TP),
                )
            ),
        ],
        in_specs=[SMEM] + [HBM] * 5,
        scratch=[
            pltpu.VMEM((32, tiles), jnp.int32),
            pltpu.VMEM((tiles * shots, TP), BF16),
            pltpu.VMEM((tiles * shots, TP), F32),
            pltpu.SemaphoreType.DMA((5,)),
        ],
    )
    lead = cross(sent[-1], owners // 2, owners)
    own, other, far = exchange(sent[:chips], sent[2 * chips], owners, META)
    last = chips // 2 - 1
    early = [own, other, *far[:last], *far[last + 1 :], far[last]]
    own, other, far = exchange(sent[chips : 2 * chips], sent[2 * chips + 1], owners, 0)
    near, far = far[:last] + far[last + 1 :], far[last : last + 1]
    pick, live, kern, cyc0, mask = call(
        lambda *refs: gather_kernel(owners, capacity, *refs),
        [
            jax.ShapeDtypeStruct((SLOTS, rows), BF16),
            jax.ShapeDtypeStruct((rows, TP), BF16),
            jax.ShapeDtypeStruct((rows, TP), F32),
            jax.ShapeDtypeStruct((SLOTS, TP), F32),
            jax.ShapeDtypeStruct((SLOTS, TP), F32),
        ],
        [*early, pltpu.with_memory_space_constraint(interp_weights, pltpu.HBM)],
        in_specs=[VMEM] * len(early) + [HBM],
        scratch=[pltpu.VMEM(interp_weights.shape, BF16), pltpu.SemaphoreType.DMA],
        flops=2 * 10**9,
    )
    after = lax.ppermute(cyc0, "shot", [((i + 1) % ring, i) for i in range(ring)])
    spec, scale = call(
        scale_kernel,
        [
            jax.ShapeDtypeStruct((HALF * Q_DEV, 2 * TP), F32),
            jax.ShapeDtypeStruct((SLOTS, TP), F32),
        ],
        [cyc0, mask, table],
        flops=10**9,
    )
    part, after = call(
        lambda *refs: partial_kernel(capacity, shots - 1, *refs),
        [
            jax.ShapeDtypeStruct((SLOTS, (shots - 1) * TP), F32),
            jax.ShapeDtypeStruct((HALF * Q_DEV, 2 * TP), F32),
        ],
        [own, other, *near, interp_weights, pick, live, kern, after, table],
        flops=10**9,
    )
    return call(
        lambda *refs: correlate_kernel(capacity, *refs),
        jax.ShapeDtypeStruct((shots, Q_DEV, ANG), F32),
        [lead, *far, interp_weights, pick, live, kern, part, spec, after, scale, table],
        out_specs=HBM,
        scratch=[
            pltpu.VMEM((shots, Q_DEV, ANG), F32),
            pltpu.SemaphoreType.DMA((shots,)),
        ],
    )


def solution(mesh):
    owners = mesh.shape["blk"]
    assert owners & (owners - 1) == 0
    placed = (P("blk", "shot", None), P("blk"), P("blk"), P("blk"), P("blk"), P())
    return jax.shard_map(
        program, mesh=mesh, in_specs=placed, out_specs=P("shot", "blk", None), check_vma=False
    )
```

```python
import math

import jax
import jax.numpy as jnp
import ml_dtypes
import numpy as np
from jax import lax
from jax.experimental import pallas as pl
from jax.experimental.pallas import tpu as pltpu
from jax.sharding import PartitionSpec as P


ANG = 2048
TP = 128
Q_DEV = 16
NSEG = 16
HALF = NSEG // 2 + 1
SLOTS = Q_DEV * NSEG
LANES = 128
META = 8
TWIST = 2 * 2 * TP
ROOT = math.sqrt(0.5)
COS1, SIN1 = math.cos(math.pi / 8), math.sin(math.pi / 8)


F32 = jnp.float32
BF16 = jnp.bfloat16


def pieces(array, count):
    terms = []
    for _ in range(count):
        terms.append(array.astype(np.float32).astype(ml_dtypes.bfloat16))
        array = array - terms[-1].astype(np.float64)
    return terms


def dft_table():
    lane = np.arange(TP)
    angle = 2.0 * np.pi * (np.outer(lane, lane) % TP) / TP
    cosine, sine = np.cos(angle), np.sin(angle)
    factors = np.block([[cosine, sine], [-sine, cosine]])
    turn = 2.0 * np.pi * np.outer(np.arange(NSEG), lane) / ANG
    twist = np.concatenate([np.cos(turn), np.sin(turn)], axis=1)
    return np.concatenate(pieces(factors, 2) + pieces(twist, 3), axis=0)


def split(value):
    high = value.astype(BF16)
    return high, (value - high.astype(F32)).astype(BF16)


def dot(a, b):
    return jnp.dot(a, b, preferred_element_type=F32)


def dot_rows(a, b):
    return lax.dot_general(a, b, (((1,), (1,)), ((), ())), preferred_element_type=F32)


def iota(shape, axis):
    return lax.broadcasted_iota(jnp.int32, shape, axis)


def factor_dot(value, table_ref):
    high, low = split(value)
    table_high, table_low = table_ref[: 2 * TP, :], table_ref[2 * TP : TWIST, :]
    return dot(high, table_high) + (dot(high, table_low) + dot(low, table_high))


def twist_of(table_ref):
    terms = [
        table_ref[TWIST + i * NSEG : TWIST + (i + 1) * NSEG, :].astype(F32) for i in range(3)
    ]
    whole = terms[0] + (terms[1] + terms[2])
    return [(whole[k : k + 1, :TP], whole[k : k + 1, TP:]) for k in range(HALF)]


def real_dft(x):
    a = [x[j] + x[j + 8] for j in range(8)]
    b = [x[j] - x[j + 8] for j in range(8)]
    c = [None] + [b[j] - b[8 - j] for j in range(1, 4)]
    s = [None] + [b[j] + b[8 - j] for j in range(1, 4)]
    a2 = [a[j] + a[j + 4] for j in range(4)]
    b2 = [a[j] - a[j + 4] for j in range(4)]
    real, imag = [None] * 9, [None] * 9
    even, odd = a2[0] + a2[2], a2[1] + a2[3]
    real[0], real[8] = even + odd, even - odd
    real[4], imag[4] = a2[0] - a2[2], a2[1] - a2[3]
    left, right = ROOT * (b2[1] - b2[3]), ROOT * (b2[1] + b2[3])
    real[2], real[6] = b2[0] + left, b2[0] - left
    imag[2], imag[6] = right + b2[2], right - b2[2]
    side, rise = ROOT * c[2], ROOT * s[2]
    for k, even, odd, odd_sine, even_sine in (
        (1, b[0] + side, COS1 * c[1] + SIN1 * c[3], SIN1 * s[1] + COS1 * s[3], rise + b[4]),
        (3, b[0] - side, SIN1 * c[1] - COS1 * c[3], COS1 * s[1] - SIN1 * s[3], rise - b[4]),
    ):
        real[k], real[8 - k] = even + odd, even - odd
        imag[k], imag[8 - k] = odd_sine + even_sine, odd_sine - even_sine
    return real, imag


def real_inverse(p, n):
    u1, v1, u3, v3 = p[1] + p[7], p[1] - p[7], p[3] + p[5], p[3] - p[5]
    x1, y1, x3, y3 = n[1] + n[7], n[1] - n[7], n[3] + n[5], n[3] - n[5]
    a = [u1 + u3, COS1 * v1 + SIN1 * v3, ROOT * (u1 - u3), SIN1 * v1 - COS1 * v3]
    b = [None, SIN1 * x1 + COS1 * x3, ROOT * (y1 + y3), COS1 * x1 - SIN1 * x3, y1 - y3]
    odd = [a[0], a[1] - b[1], a[2] - b[2], a[3] - b[3], -b[4]]
    odd += [-a[3] - b[3], -a[2] - b[2], -a[1] - b[1]]
    zero, eight = 0.5 * p[0], 0.5 * p[8]
    e0, e1 = zero + eight, zero - eight
    c, d = p[2] + p[6], ROOT * (p[2] - p[6])
    e, f = ROOT * (n[2] + n[6]), n[2] - n[6]
    up, down = e0 + p[4], e0 - p[4]
    left, right = e1 - n[4], e1 + n[4]
    near, far = d - e, d + e
    even = [up + c, left + near, down - f, right - far, up - c, left - near, down + f, right + far]
    return [even[m] + odd[m] for m in range(8)] + [even[m] - odd[m] for m in range(8)]


def slabs(value, count):
    return [value[k * Q_DEV : (k + 1) * Q_DEV, :] for k in range(count)]


def spectrum(cycles, table_ref):
    twist = twist_of(table_ref)
    reals, imags = [], []
    for cycle in cycles:
        real, imag = real_dft(slabs(cycle, NSEG))
        for k, (cosine, sine) in enumerate(twist):
            if k == 0:
                reals.append(real[k])
                imags.append(jnp.zeros_like(real[k]))
            elif imag[k] is None:
                reals.append(real[k] * cosine)
                imags.append(real[k] * sine)
            else:
                reals.append(real[k] * cosine - imag[k] * sine)
                imags.append(imag[k] * cosine + real[k] * sine)
    grid = jnp.concatenate(
        [jnp.concatenate(reals, axis=0), jnp.concatenate(imags, axis=0)], axis=1
    )
    return factor_dot(grid, table_ref)


def correlation(grid, twist):
    real, imag = slabs(grid[:, :TP], HALF), slabs(grid[:, TP:], HALF)
    p, n = [real[0]], [None]
    for k in range(1, HALF):
        cosine, sine = twist[k]
        p.append(real[k] * cosine - imag[k] * sine)
        n.append(None if k == HALF - 1 else real[k] * sine + imag[k] * cosine)
    return real_inverse(p, n)


def pack_kernel(owners, capacity, me_ref, owner_hbm, place_hbm, kern_hbm, len_hbm, pix_hbm, *rest):
    chips = owners // 2
    head = far_order(owners)[0] // 2
    keep = [j for j in range(chips) if j != head]
    first, later = dict(zip(keep, rest)), dict(zip(keep, rest[chips - 1 :]))
    swap_first, swap_later, ahead, ints, pix, wide, sems = rest[2 * chips - 2 :]
    tiles = ints.shape[1]
    shots = pix.shape[0] // tiles
    first_rows, later_rows = capacity + META, (shots - 1) * capacity
    copies = [
        pltpu.make_async_copy(source, ints.at[pl.ds(8 * i, 1), :], sems.at[i])
        for i, source in enumerate((owner_hbm, place_hbm, kern_hbm, len_hbm))
    ]
    copies.append(pltpu.make_async_copy(pix_hbm, pix, sems.at[4]))
    for copy in copies:
        copy.start()
    before = (iota((tiles, tiles), 0) < iota((tiles, tiles), 1)).astype(F32).astype(BF16)
    for copy in copies[:4]:
        copy.wait()
    owner = ints[0:1, :]
    mine = (iota((owners, tiles), 0) == owner).astype(F32)
    rank = jnp.sum(dot(mine.astype(BF16), before) * mine, axis=0, keepdims=True)
    slot = (owner ^ me_ref[0]) * LANES + rank.astype(jnp.int32)
    place = ints[8:9, :]
    meta = jnp.concatenate(
        [
            ((place % NSEG) * Q_DEV + place // NSEG).astype(F32),
            (ints[16:17, :] + 1).astype(F32),
            ints[24:25, :].astype(F32),
            jnp.zeros((1, tiles), F32),
        ],
        axis=0,
    )
    blank = jnp.zeros_like(meta)
    metas = [
        jnp.concatenate(pair, axis=0).astype(BF16) for pair in ((meta, blank), (blank, meta))
    ]
    placing = [
        (iota((LANES, tiles), 0) + d * LANES == slot).astype(F32).astype(BF16)
        for d in range(owners)
    ]
    tags = [dot_rows(metas[d % 2], placing[d]).astype(BF16) for d in range(owners)]
    copies[4].wait()
    wide[...] = pix[...].astype(F32)
    pixels = jnp.concatenate(
        [wide[pl.ds(s, tiles, stride=shots), :].astype(BF16) for s in range(shots)], axis=1
    )
    for d in range(owners):
        sent = dot(placing[d][:capacity], pixels).astype(BF16)
        j = d // 2
        if d % 2:
            near, far, at, to = swap_first, swap_later, j * first_rows, j * later_rows
        elif j == head:
            near, far, at, to = ahead, ahead, 0, first_rows
        else:
            near, far, at, to = first[j], later[j], 0, 0
        near[at : at + capacity, :] = sent[:, :TP]
        near[at + capacity : at + first_rows, :] = tags[d]
        for s in range(1, shots):
            start = to + (s - 1) * capacity
            far[start : start + capacity, :] = sent[:, s * TP : (s + 1) * TP]


def merge_kernel(chips, head, shared, *refs):
    own, other, outs = list(refs[: chips - 2]), refs[chips - 2], refs[chips - 1 :]
    size = other.shape[0] // chips
    body = size - shared
    for j in range(1, chips):
        start, out = j * size, outs[j - 1]
        if j == head:
            out[...] = other[start : start + size, :]
            continue
        block = own.pop(0)
        out[:body, :] = block[:body, :]
        out[body : 2 * body, :] = other[start : start + body, :]
        if shared:
            out[2 * body :, :] = block[body:, :] + other[start + body : start + size, :]


def interpolate(pixels, kern, weights_ref):
    kernels = weights_ref.shape[0]
    weights = jnp.concatenate([weights_ref[k] for k in range(kernels)], axis=1)
    every = dot(pixels, weights)
    value = every[:, :TP]
    for k in range(1, kernels):
        value = jnp.where(kern == k + 1.0, every[:, k * TP : (k + 1) * TP], value)
    return value


def scatter(pick, values):
    halves = [half for value in values for half in split(value)]
    sums = dot(pick, jnp.concatenate(halves, axis=1))
    return [
        sums[:, 2 * s * TP : (2 * s + 1) * TP] + sums[:, (2 * s + 1) * TP : (2 * s + 2) * TP]
        for s in range(len(values))
    ]


def gather_kernel(capacity, spots, *refs):
    weights_hbm, pick_ref, live_ref, kern_ref, cyc0_ref, mask_ref, weights_ref, sem = refs[-8:]
    copy = pltpu.make_async_copy(weights_hbm, weights_ref, sem)
    copy.start()
    owners = len(spots)
    got = [refs[i].at[pl.ds(start, capacity), :] for i, start, _ in spots]
    metas = [
        refs[i][row : row + META, :].astype(F32)[4 * (b % 2) : 4 * (b % 2) + 4]
        for b, (i, _, row) in enumerate(spots)
    ]
    group = math.gcd(owners, 4)
    for base in range(0, owners, group):
        tags = jnp.concatenate([m[1:3] for m in metas[base : base + group]], axis=0)
        if group < 4:
            tags = jnp.concatenate([tags, jnp.zeros((8 - 2 * group, LANES), F32)], axis=0)
        tags = jnp.transpose(tags)
        for i in range(group):
            rows = slice((base + i) * capacity, (base + i + 1) * capacity)
            kern_ref[rows, :] = jnp.broadcast_to(
                tags[:capacity, 2 * i : 2 * i + 1], (capacity, TP)
            )
            live = iota((capacity, TP), 1).astype(F32) < tags[:capacity, 2 * i + 1 : 2 * i + 2]
            live_ref[rows, :] = jnp.where(live, 1.0, 0.0).astype(BF16)
    place = [jnp.where(m[1:2] > 0.5, m[0:1], -1.0)[:, :capacity] for m in metas]
    place = jnp.broadcast_to(jnp.concatenate(place, axis=1), (SLOTS, owners * capacity))
    slot = iota((SLOTS, owners * capacity), 0).astype(F32).astype(BF16)
    one = jnp.ones(slot.shape, BF16)
    pick_ref[...] = jnp.where(slot == place.astype(BF16), one, jnp.zeros_like(one))
    live, kern = live_ref[...], kern_ref[...]
    pixels = jnp.concatenate([g[...] for g in got], axis=0) * live
    copy.wait()
    cyc0_ref[...], mask_ref[...] = scatter(
        pick_ref[...],
        [interpolate(pixels, kern, weights_ref), interpolate(live, kern, weights_ref)],
    )


def scale_kernel(cyc0_ref, mask_ref, table_ref, spec_ref, scale_ref):
    spec = spectrum([cyc0_ref[...], mask_ref[...]], table_ref)
    rows = spec_ref.shape[0]
    spec_ref[...] = spec[:rows]
    real, imag = spec[rows:, :TP], spec[rows:, TP:]
    power = jnp.concatenate([real * real + imag * imag, jnp.zeros_like(real)], axis=1)
    corr = correlation(factor_dot(power, table_ref), twist_of(table_ref))
    least = jnp.maximum(corr[0][:, :1] * (0.01 * 2.0 / ANG), 1.0)
    for m in range(NSEG):
        whole = jnp.maximum(corr[m] * (2.0 / ANG), least)
        scale_ref[m * Q_DEV : (m + 1) * Q_DEV, :] = (2.0 / ANG) / whole


def late_cycles(blocks, live_ref, kern_ref, pick_ref, weights_ref, first):
    count = sum(ref.shape[0] for ref in blocks[0])
    capacity = count // len(blocks[0])
    rows = slice(first, first + capacity * len(blocks))
    live, kern = live_ref[rows, :], kern_ref[rows, :]
    values = [
        interpolate(
            jnp.concatenate([block[s][...] for block in blocks], axis=0) * live, kern, weights_ref
        )
        for s in range(len(blocks[0]))
    ]
    return scatter(pick_ref[:, rows], values)


def late_blocks(refs, capacity, shots, spots):
    return [
        [refs[i].at[pl.ds(start + s * capacity, capacity), :] for s in range(shots)]
        for i, start in spots
    ]


def partial_kernel(capacity, shots, spots, *refs):
    weights_ref, pick_ref, live_ref, kern_ref, part_ref = refs[-5:]
    blocks = late_blocks(refs, capacity, shots, spots)
    cycles = late_cycles(blocks, live_ref, kern_ref, pick_ref, weights_ref, 0)
    for s, cycle in enumerate(cycles):
        part_ref[:, s * TP : (s + 1) * TP] = cycle


def after_kernel(next_ref, table_ref, spec_ref):
    spec_ref[...] = spectrum([next_ref[...]], table_ref)


def correlate_kernel(capacity, spots, *refs):
    (weights_ref, pick_ref, live_ref, kern_ref, part_ref, spec_ref, next_ref, scale_ref, table_ref,
     out_hbm, out, sems) = refs[-12:]
    shots = out.shape[0]
    blocks = late_blocks(refs, capacity, shots - 1, spots)
    first = live_ref.shape[0] - capacity * len(blocks)
    cycles = late_cycles(blocks, live_ref, kern_ref, pick_ref, weights_ref, first)
    cycles = [c + part_ref[:, s * TP : (s + 1) * TP] for s, c in enumerate(cycles)]
    spec = jnp.concatenate([spec_ref[...], spectrum(cycles, table_ref), next_ref[...]], axis=0)
    rows = HALF * Q_DEV
    diff = spec[: shots * rows] - spec[rows:]
    spec = spec[: shots * rows]
    real, imag = spec[:, :TP], spec[:, TP:]
    diff_real, diff_imag = diff[:, :TP], diff[:, TP:]
    cross = jnp.concatenate(
        [real * diff_real + imag * diff_imag, real * diff_imag - imag * diff_real], axis=1
    )
    grid = factor_dot(cross, table_ref)
    twist = twist_of(table_ref)
    copies = []
    for s in range(shots):
        corr = correlation(grid[s * rows : (s + 1) * rows], twist)
        for m in range(NSEG):
            out[s, :, m * TP : (m + 1) * TP] = corr[m] * scale_ref[m * Q_DEV : (m + 1) * Q_DEV, :]
        copies.append(pltpu.make_async_copy(out.at[s], out_hbm.at[s], sems.at[s]))
        copies[-1].start()
    for copy in copies:
        copy.wait()


VMEM = pl.BlockSpec(memory_space=pltpu.VMEM)
SMEM = pl.BlockSpec(memory_space=pltpu.SMEM)
HBM = pl.BlockSpec(memory_space=pltpu.HBM)


def call(body, outs, operands, in_specs=None, out_specs=None, scratch=(), flops=0, limit=20 << 20):
    return pl.pallas_call(
        body,
        out_shape=outs,
        in_specs=in_specs or [VMEM] * len(operands),
        out_specs=out_specs or jax.tree.map(lambda _: VMEM, outs),
        scratch_shapes=list(scratch),
        compiler_params=pltpu.CompilerParams(vmem_limit_bytes=limit),
        cost_estimate=pl.CostEstimate(flops=flops, bytes_accessed=1 << 20, transcendentals=0),
    )(*operands)


def far_order(owners):
    return sorted(range(2, owners, 2), key=lambda d: (d < owners // 2, -d))


def cross(block, d, owners):
    return lax.ppermute(block, "blk", [(i, i ^ d) for i in range(owners)])


def exchange(own, swap, owners, shared):
    chips, order = owners // 2, far_order(owners)
    head = order[0] // 2
    other = cross(swap, 1, owners)
    size = swap.shape[0] // chips
    merged = call(
        lambda *refs: merge_kernel(chips, head, shared, *refs),
        [
            jax.ShapeDtypeStruct((size if j == head else 2 * size - shared, TP), BF16)
            for j in range(1, chips)
        ],
        [*(own[j] for j in range(1, chips) if j != head), other],
    )
    return other, {d: cross(merged[d // 2 - 1], d, owners) for d in order}


def program(intensities, tile_owner, tile_place, tile_kernel, mask_len, interp_weights):
    owners = lax.axis_size("blk")
    chips = owners // 2
    order, tail = far_order(owners), owners // 2
    head = order[0]
    keep = [j for j in range(chips) if 2 * j != head]
    ring = lax.axis_size("shot")
    tiles, shots, _ = intensities.shape
    capacity = -(-(3 * tiles // owners) // 16) * 16
    rows = owners * capacity
    table = jnp.asarray(dft_table())
    me = lax.axis_index("blk").astype(jnp.int32).reshape(1)
    sent = call(
        lambda *refs: pack_kernel(owners, capacity, *refs),
        [jax.ShapeDtypeStruct((capacity + META, TP), BF16)] * (chips - 1)
        + [jax.ShapeDtypeStruct(((shots - 1) * capacity, TP), BF16)] * (chips - 1)
        + [jax.ShapeDtypeStruct((chips * (capacity + META), TP), BF16)]
        + [jax.ShapeDtypeStruct((chips * (shots - 1) * capacity, TP), BF16)]
        + [jax.ShapeDtypeStruct((shots * capacity + META, TP), BF16)],
        [
            me,
            *(
                pltpu.with_memory_space_constraint(v, pltpu.HBM)
                for v in (
                    tile_owner.reshape(1, tiles),
                    tile_place.reshape(1, tiles),
                    tile_kernel.reshape(1, tiles),
                    mask_len.reshape(1, tiles),
                    intensities.reshape(tiles * shots, TP),
                )
            ),
        ],
        in_specs=[SMEM] + [HBM] * 5,
        scratch=[
            pltpu.VMEM((32, tiles), jnp.int32),
            pltpu.VMEM((tiles * shots, TP), BF16),
            pltpu.VMEM((tiles * shots, TP), F32),
            pltpu.SemaphoreType.DMA((5,)),
        ],
    )
    first, later = dict(zip(keep, sent)), dict(zip(keep, sent[chips - 1 :]))
    swap_first, swap_later, ahead = sent[-3:]
    ahead = cross(ahead, head, owners)
    other_first, far_first = exchange(first, swap_first, owners, META)
    other_later, far_later = exchange(later, swap_later, owners, 0)
    distant = [d for d in order if d not in (head, tail)] + [tail]
    early = [first[0], other_first, ahead, far_first[head]] + [far_first[d] for d in distant]
    early_spots = [(i, 0, capacity) for i in range(4)]
    early_spots += [
        (4 + i, core * capacity, 2 * capacity) for i in range(len(distant)) for core in range(2)
    ]
    near = [later[0], other_later, ahead, far_later[head]] + [far_later[d] for d in distant[:-1]]
    near_spots = [(0, 0), (1, 0), (2, capacity + META), (3, 0)]
    both = [(0, 0), (0, (shots - 1) * capacity)]
    near_spots += [(4 + i, start) for i in range(len(distant) - 1) for _, start in both]
    pick, live, kern, cyc0, mask = call(
        lambda *refs: gather_kernel(capacity, early_spots, *refs),
        [
            jax.ShapeDtypeStruct((SLOTS, rows), BF16),
            jax.ShapeDtypeStruct((rows, TP), BF16),
            jax.ShapeDtypeStruct((rows, TP), F32),
            jax.ShapeDtypeStruct((SLOTS, TP), F32),
            jax.ShapeDtypeStruct((SLOTS, TP), F32),
        ],
        [*early, pltpu.with_memory_space_constraint(interp_weights, pltpu.HBM)],
        in_specs=[VMEM] * len(early) + [HBM],
        scratch=[pltpu.VMEM(interp_weights.shape, BF16), pltpu.SemaphoreType.DMA],
        flops=2 * 10**9,
    )
    after = lax.ppermute(cyc0, "shot", [((i + 1) % ring, i) for i in range(ring)])
    spec, scale = call(
        scale_kernel,
        [
            jax.ShapeDtypeStruct((HALF * Q_DEV, 2 * TP), F32),
            jax.ShapeDtypeStruct((SLOTS, TP), F32),
        ],
        [cyc0, mask, table],
        flops=10**9,
    )
    part = call(
        lambda *refs: partial_kernel(capacity, shots - 1, near_spots, *refs),
        jax.ShapeDtypeStruct((SLOTS, (shots - 1) * TP), F32),
        [*near, interp_weights, pick, live, kern],
        flops=10**9,
    )
    after = call(
        after_kernel, jax.ShapeDtypeStruct((HALF * Q_DEV, 2 * TP), F32), [after, table], flops=10**8
    )
    return call(
        lambda *refs: correlate_kernel(capacity, both, *refs),
        jax.ShapeDtypeStruct((shots, Q_DEV, ANG), F32),
        [far_later[tail], interp_weights, pick, live, kern, part, spec, after, scale, table],
        out_specs=HBM,
        scratch=[
            pltpu.VMEM((shots, Q_DEV, ANG), F32),
            pltpu.SemaphoreType.DMA((shots,)),
        ],
    )


def solution(mesh):
    owners = mesh.shape["blk"]
    assert owners & (owners - 1) == 0
    placed = (P("blk", "shot", None), P("blk"), P("blk"), P("blk"), P("blk"), P())
    return jax.shard_map(
        program, mesh=mesh, in_specs=placed, out_specs=P("shot", "blk", None), check_vma=False
    )
```
